256 devices in a mesh: grp: 2 (over core), dp: 32 (over x, z_hi, y), mp: 4 (over z_lo).
Axes of the slice: x: 4, y: 4, z: 8 (z_hi: 2, z_lo: 4; z = z_hi * 4 + z_lo), core: 2. Of those that a mesh axis runs over, the one named last changes fastest.
Arguments:
- states: bfloat16 [2, 64, 128, 4096], P('grp', 'dp'), may hold values from -6 to 6
- loss_grad: bfloat16 [64, 128, 4096], P('dp'), may hold values from -6 to 6
- gains: float32 [2, 4096], P('grp'), may hold values from 0.25 to 1.75
- w_param: bfloat16 [2, 4096, 2048], P('grp', 'dp', 'mp'), may hold values from -0.0234375 to 0.0234375, as said below
- w_fixed: bfloat16 [2, 4096, 2048], P('grp', 'dp', 'mp'), may hold values from -0.09375 to 0.09375
- probes: bfloat16 [2, 4096, 2, 2048], P('grp', 'dp', None, 'mp'), may hold values from -0.0234375 to 0.0234375, as said below
Outputs:
- hv: bfloat16 [2, 4096, 2, 2048], P('grp', 'dp', None, 'mp')
The draws below stay inside these ranges and needn't reach their ends.
Inputs may be any that keep to these rules, and one draw needn't show every extreme that they name: `w_param`: independent entries of mean 0. `probes`: independent entries of mean 0.
All inputs are finite; a program needn't handle non-finite values.
Results may differ from the reference program's by a relative error of at most 0.025.
Values may be sent and summed in bfloat16 or wider, within the bound.
No kernel may reach another device: no remote copies, remote signals or barrier semaphores. Data moves between devices by JAX's collectives and lax.ppermute only.
A program may use at most 128 MiB of HBM per device.

```python
import jax
import jax.numpy as jnp
from jax import lax

D = 4096
HEAD = 256
HEADS = 8
PROBES = 2
LEN = 128
SEQ_DEV = 2
SEQS = 64
HD = 2048
N_DP = 32


def folded_entries(key, shape):
    spread = float(D) ** (-0.5) * float(HEAD) ** (-0.25)
    unit = jnp.clip(jax.random.normal(key, shape, jnp.float32), -6.0, 6.0)
    return unit * spread


def draw_w_param(key, part):
    return folded_entries(jax.random.fold_in(key, 11), (2, D, HEADS * HEAD)).astype(jnp.bfloat16)


def draw_probes(key, part):
    return folded_entries(jax.random.fold_in(key, 23), (2, D, PROBES, HEADS * HEAD)).astype(jnp.bfloat16)


def level_of(own_key, shape, shards, least, top_value):
    level = 1.0
    for axis_at, blocks in shards:
        heights = jax.random.uniform(jax.random.fold_in(jax.random.fold_in(own_key, 6), axis_at), (blocks,), jnp.float32, least / len(shards), top_value / len(shards))
        level = level * jnp.repeat(jnp.exp(heights), shape[axis_at] // blocks).reshape((-1,) + (1,) * (len(shape) - 1 - axis_at))
    return level


def centred(stream_key, shape, width, reach, shards=(), kind=jnp.bfloat16):
    entries = width * jax.random.normal(stream_key, shape, jnp.float32)
    if shards:
        entries = entries * level_of(stream_key, shape, shards, -0.22, 0.18)
    return jnp.clip(entries, -reach, reach).astype(kind)


def setup_inputs(seed: int = 0) -> dict:
    key_list = jax.random.split(jax.random.key(seed), 7)
    states = centred(key_list[0], (2, SEQS, LEN, D), 1.0, 6.0, ((0, 2), (1, 32)))
    loss_grad = centred(key_list[1], (SEQS, LEN, D), 1.0, 6.0, ((0, 32),))
    gains = jnp.clip(1.0 + 0.15 * jax.random.normal(key_list[2], (2, D), jnp.float32), 0.25, 1.75)
    w_param = draw_w_param(jax.random.fold_in(key_list[6], 71), 0)
    w_fixed = centred(key_list[4], (2, D, HD), D ** -0.5, 0.09375, ((0, 2), (1, 32), (2, 4)))
    probes = draw_probes(jax.random.fold_in(key_list[6], 71), 0)
    return dict(states=states, loss_grad=loss_grad, gains=gains, w_param=w_param, w_fixed=w_fixed, probes=probes)


EPS = 1e-06

def normalize(rows, gain):
    values = rows.astype(jnp.float32)
    scale = lax.rsqrt(lax.optimization_barrier(jnp.mean(values * values, axis=-1, keepdims=True)) + EPS)
    return (values * scale * gain).astype(jnp.bfloat16)

def attention_loss(query, keys, values, out_grad, scale, weight):
    scores = jnp.einsum('sihe,sjhe->shij', query, keys) * scale
    probs = jax.nn.softmax(scores, axis=-1)
    mixing = jnp.einsum('sihe,sjhe->shij', out_grad, values)
    return jnp.sum(probs * mixing) * weight

def curvature(query, keys, values, out_grad, t_query, t_keys, scale, weight):

    def grads(q_arg, k_arg):
        return jax.grad(attention_loss, argnums=(0, 1))(q_arg, k_arg, values, out_grad, scale, weight)

    def along(a_dir, b_dir):
        return jax.jvp(grads, (query, keys), (a_dir, b_dir))[1]
    return jax.vmap(along)(t_query, t_keys)

def reference(states, loss_grad, gains, w_param, w_fixed, probes):
    rows = SEQS * LEN
    heads_split = (SEQS, LEN, HEADS, HEAD)
    normed = [normalize(states[g].reshape(rows, D), gains[g]) for g in range(2)]
    proj = [jnp.dot(normed[g], w_param[g], preferred_element_type=jnp.float32).astype(jnp.bfloat16) for g in range(2)]
    tang = [jnp.einsum('rd,dpe->rpe', normed[g].astype(jnp.float32), probes[g].astype(jnp.float32)).astype(jnp.bfloat16) for g in range(2)]
    values = jnp.dot(normed[0], w_fixed[0], preferred_element_type=jnp.float32).astype(jnp.bfloat16)
    outgrad = jnp.dot(loss_grad.reshape(rows, D), w_fixed[1], preferred_element_type=jnp.float32).astype(jnp.bfloat16)

    def heads_of(x):
        return x.astype(jnp.float32).reshape(heads_split)

    def probe_heads(x):
        return jnp.moveaxis(x.astype(jnp.float32).reshape(SEQS, LEN, PROBES, HEADS, HEAD), 2, 0)
    scale = 1.0
    weight = float(SEQS * LEN) ** (-0.5)
    d_query, d_keys = curvature(heads_of(proj[1]), heads_of(proj[0]), heads_of(values), heads_of(outgrad), probe_heads(tang[1]), probe_heads(tang[0]), scale, weight)

    def back_rows(x):
        return jnp.moveaxis(x, 0, 2).reshape(rows, PROBES, HD).astype(jnp.bfloat16)
    d_query = back_rows(d_query)
    d_keys = back_rows(d_keys)

    def block_sum(left, right):
        left_blocks = left.reshape(N_DP, SEQ_DEV * LEN, D)
        right_blocks = right.reshape(N_DP, SEQ_DEV * LEN, PROBES, HD)

        def step(total, pair):
            part = jnp.einsum('rd,rpe->dpe', pair[0].astype(jnp.float32), pair[1].astype(jnp.float32))
            part = lax.optimization_barrier(part.astype(jnp.bfloat16)).astype(jnp.float32)
            return (total + part, None)
        total, _ = lax.scan(step, jnp.zeros((D, PROBES, HD), jnp.float32), (left_blocks, right_blocks))
        return total.astype(jnp.bfloat16)
    return jnp.stack([block_sum(normed[0], d_keys), block_sum(normed[1], d_query)])
```

```python
import numpy as np
import jax
import jax.numpy as jnp
from jax import lax
from jax.experimental import pallas as pl
from jax.experimental.pallas import tpu as pltpu
from jax.sharding import Mesh, PartitionSpec as P

HEAD = 256
EPS = 1e-06
BF = jnp.bfloat16
F32 = jnp.float32
NX, NY, NZ, NM = 4, 4, 2, 4
BLK = 128
OFFS = (0, -1, 1, 2)


def position_table():
    rows = []
    for grp in range(2):
        for x in range(NX):
            for zh in range(NZ):
                for y in range(NY):
                    for mp in range(NM):
                        row = []
                        for c in range(2):
                            for o2 in OFFS:
                                for o1 in OFFS:
                                    ox, oy = (o1, o2) if grp == 0 else (o2, o1)
                                    xx, yy = (x + ox) % NX, (y + oy) % NY
                                    row.append(xx * 8 + (zh ^ c) * 4 + yy)
                        rows.append(row + [grp, mp])
    return np.asarray(rows, np.int32)


def plane_perm(first, step):
    pairs = []
    for g in range(2):
        for x in range(NX):
            for y in range(NY):
                along_x = (g == 0) == first
                tx, ty = ((x + step) % NX, y) if along_x else (x, (y + step) % NY)
                pairs.append((g * 16 + x * 4 + y, g * 16 + tx * 4 + ty))
    return pairs


def pp1(v, step):
    return lax.ppermute(v, ("grp", "x", "y"), plane_perm(True, step))


def pp2(v, step):
    return lax.ppermute(v, ("grp", "x", "y"), plane_perm(False, step))


def ppz(v, step):
    return lax.ppermute(v, ("zh", "mp"), [(i, (i + step) % 8) for i in range(8)])


def pp_pair(v):
    return lax.ppermute(v, "zh", [(0, 1), (1, 0)])


SMEM = pl.BlockSpec(memory_space=pltpu.SMEM)
VMEM = pl.BlockSpec(memory_space=pltpu.VMEM)


def norm_rows(tab, rows, gains, out, at):
    total = jnp.zeros((rows.shape[0], BLK), F32)
    for b in range(32):
        piece = rows[:, b * BLK : (b + 1) * BLK].astype(F32)
        total = total + piece * piece
    scale = lax.rsqrt(jnp.sum(total, axis=-1, keepdims=True) * (1.0 / (32 * BLK)) + EPS)
    for b in range(32):
        src = pl.ds(pl.multiple_of(tab[b] * BLK, BLK), BLK)
        out[at, b * BLK : (b + 1) * BLK] = (rows[:, src].astype(F32) * scale * gains[:, src]).astype(BF)


def norm_own_kernel(tab, rows, other, gains, out, src_out):
    norm_rows(tab, rows, gains, out, slice(None))

    @pl.when(tab[32] == 0)
    def _():
        src_out[...] = out[...]

    @pl.when(tab[32] != 0)
    def _():
        for b in range(32):
            src = pl.ds(pl.multiple_of(tab[b] * BLK, BLK), BLK)
            src_out[:, b * BLK : (b + 1) * BLK] = other[:, src]


def norm_own(tab, rows, other, gains):
    n, width = rows.shape
    step = 32
    spec = pl.BlockSpec((step, width), lambda i: (i, 0))
    return pl.pallas_call(
        norm_own_kernel,
        grid=(n // step,),
        in_specs=[SMEM, spec, spec, pl.BlockSpec((1, width), lambda i: (0, 0))],
        out_specs=[spec, spec],
        out_shape=[jax.ShapeDtypeStruct((n, width), BF)] * 2,
        name="norm_own",
    )(tab, rows, other, gains)


def norm_pair_kernel(tab, gains, p1, p2, p3, m1, m2, m3, f0, f1, out):
    mp = tab[33]
    sources = {-3: (m1, m1), -2: (m2, m2), -1: (m3, m3), 0: (f0, f1), 1: (p3, p3), 2: (p2, p2), 3: (p1, p1)}
    for d, pair in sources.items():

        @pl.when((mp + d >= 0) & (mp + d < NM))
        def _():
            for s in range(2):
                at = pl.ds(pl.multiple_of(s * 128 + (mp + d) * 32, 32), 32)
                ref = pair[s].at[s] if d != 0 else pair[s].at[0]
                norm_rows(tab, ref, gains, out, at)


def norm_pair(tab, gains, pieces):
    width = gains.shape[1]
    return pl.pallas_call(
        norm_pair_kernel,
        in_specs=[SMEM] + [VMEM] * 9,
        out_specs=VMEM,
        out_shape=jax.ShapeDtypeStruct((256, width), BF),
        name="norm_pair",
    )(tab, gains, *pieces)


def dots(rows, weights, base):
    total = None
    for w in weights:
        k = w.shape[0]
        part = jnp.dot(rows[:, base : base + k], w[...], preferred_element_type=F32)
        total = part if total is None else total + part
        base += k
    return total


def proj_own_kernel(n, s, *refs):
    weights, (out, sent) = refs[:10], refs[10:]
    j = pl.program_id(0)

    @pl.when(j == 0)
    def _():
        sent[...] = dots(s, weights, 0).astype(BF)

    @pl.when(j == 1)
    def _():
        out[...] = dots(s, weights, 0).astype(BF)

    @pl.when(j > 1)
    def _():
        out[...] = dots(n, weights, 0).astype(BF)


def proj_own(n, s, weights):
    rows, width = n.shape
    whole = pl.BlockSpec((rows, width), lambda j: (0, 0))
    return pl.pallas_call(
        proj_own_kernel,
        grid=(5,),
        in_specs=[whole, whole] + [pl.BlockSpec((w.shape[0], HEAD), lambda j: (0, j)) for w in weights],
        out_specs=[
            pl.BlockSpec((rows, HEAD), lambda j: (0, jnp.maximum(j - 1, 0))),
            pl.BlockSpec((rows, HEAD), lambda j: (0, 0)),
        ],
        out_shape=[jax.ShapeDtypeStruct((rows, 4 * HEAD), BF), jax.ShapeDtypeStruct((rows, HEAD), BF)],
        name="proj_own",
    )(n, s, *weights)


def proj_pair_kernel(n, *refs):
    weights, out = refs[:10], refs[10]
    out[...] = dots(n, weights, 0).astype(BF)


def proj_pair(n, weights):
    rows, width = n.shape
    return pl.pallas_call(
        proj_pair_kernel,
        grid=(3,),
        in_specs=[pl.BlockSpec((rows, width), lambda j: (0, 0))]
        + [pl.BlockSpec((w.shape[0], HEAD), lambda j: (0, j + 2)) for w in weights],
        out_specs=pl.BlockSpec((rows, HEAD), lambda j: (0, j)),
        out_shape=jax.ShapeDtypeStruct((rows, 3 * HEAD), BF),
        name="proj_pair",
    )(n, *weights)


NT = (((1,), (1,)), ((), ()))
TN = (((0,), (0,)), ((), ()))


def curvature(q, k, v, o, tq, tk, weight):
    dot = lambda a, b, dims: lax.dot_general(a, b, dims, preferred_element_type=F32)
    scores = dot(q, k, NT)
    top = jnp.max(scores, axis=-1, keepdims=True)
    e = jnp.exp(scores - top)
    probs = e / jnp.sum(e, axis=-1, keepdims=True)
    mixing = dot(o, v, NT)
    centred = mixing - jnp.sum(probs * mixing, axis=-1, keepdims=True)
    grad = probs * centred
    grad_b = grad.astype(BF)
    dqs, dks = [], []
    for p in range(2):
        t_scores = dot(tq[p], k, NT) + dot(q, tk[p], NT)
        t_probs = probs * (t_scores - jnp.sum(probs * t_scores, axis=-1, keepdims=True))
        t_mean = jnp.sum(t_probs * mixing, axis=-1, keepdims=True)
        t_grad = t_probs * centred - probs * t_mean
        t_b = t_grad.astype(BF)
        dq = jnp.dot(t_b, k, preferred_element_type=F32) + jnp.dot(grad_b, tk[p], preferred_element_type=F32)
        dk = dot(t_b, q, TN) + dot(grad_b, tq[p], TN)
        dqs.append((dq * weight).T.astype(BF))
        dks.append((dk * weight).T.astype(BF))
    return dqs, dks


def attention_kernel(weight, tab, own_a, got_a, own_b, got_b, v_b, o_b, keep, send):
    def tile(ref, s, j):
        return ref[s * 128 : (s + 1) * 128, j * HEAD : (j + 1) * HEAD]

    def both(key_ref, query_ref, value_of, outgrad_of, base, key_out, query_out):
        for s in range(2):
            dqs, dks = curvature(
                tile(query_ref, s, base),
                tile(key_ref, s, base),
                value_of(s),
                outgrad_of(s),
                [tile(query_ref, s, base + 1 + p) for p in range(2)],
                [tile(key_ref, s, base + 1 + p) for p in range(2)],
                weight,
            )
            for p in range(2):
                query_out[p * HEAD : (p + 1) * HEAD, s * 128 : (s + 1) * 128] = dqs[p]
                key_out[p * HEAD : (p + 1) * HEAD, s * 128 : (s + 1) * 128] = dks[p]

    @pl.when(tab[32] == 0)
    def _():
        both(own_a, got_a, lambda s: tile(own_a, s, 0), lambda s: tile(got_a, s, 0), 1, keep, send)

    @pl.when(tab[32] != 0)
    def _():
        both(got_b, own_b, lambda s: tile(v_b, s, 0), lambda s: tile(o_b, s, 0), 0, send, keep)


def attention(weight, *args):
    return pl.pallas_call(
        lambda *refs: attention_kernel(weight, *refs),
        in_specs=[SMEM] + [VMEM] * 6,
        out_specs=[VMEM, VMEM],
        out_shape=[jax.ShapeDtypeStruct((2 * HEAD, 256), BF)] * 2,
        name="attention",
    )(*args)


def outer_kernel(tab, n_a, n_b, keep, got, out):
    @pl.when(tab[32] == 0)
    def _():
        out[0] = (
            jnp.dot(keep[...], n_a[...], preferred_element_type=F32)
            + jnp.dot(got[...], n_b[...], preferred_element_type=F32)
        ).astype(BF)

    @pl.when(tab[32] != 0)
    def _():
        out[0] = (
            jnp.dot(got[...], n_a[...], preferred_element_type=F32)
            + jnp.dot(keep[...], n_b[...], preferred_element_type=F32)
        ).astype(BF)


def outer(tab, n_a, n_b, keep, got, group):
    rows = n_a.shape[0]
    wide = pl.BlockSpec((rows, 4 * BLK), lambda c: (0, c * 4 + group))
    small = pl.BlockSpec((2 * HEAD, rows), lambda c: (0, 0))
    return pl.pallas_call(
        outer_kernel,
        grid=(2,),
        in_specs=[SMEM, wide, wide, small, small],
        out_specs=pl.BlockSpec((1, 2 * HEAD, 4 * BLK), lambda c: (c, 0, 0)),
        out_shape=jax.ShapeDtypeStruct((2, 2 * HEAD, 4 * BLK), BF),
        name="outer",
    )(tab, n_a, n_b, keep, got)


def sum_first_kernel(a, b, c, d, *outs):
    total = a[...].astype(F32) + b[...].astype(F32) + c[...].astype(F32) + d[...].astype(F32)
    for i, out in enumerate(outs):
        out[...] = total[:, :, i * BLK : (i + 1) * BLK].astype(out.dtype)


def sum_first(parts):
    shape = parts[0].shape
    step = 128
    spec = pl.BlockSpec((1, step, shape[2]), lambda c, i: (c, i, 0))
    return pl.pallas_call(
        sum_first_kernel,
        grid=(shape[0], shape[1] // step),
        in_specs=[spec] * 4,
        out_specs=[pl.BlockSpec((1, step, BLK), lambda c, i: (c, i, 0))] * 4,
        out_shape=[jax.ShapeDtypeStruct((shape[0], shape[1], BLK), F32 if i == 0 else BF) for i in range(4)],
        name="sum_first",
    )(*parts)


def sum_second_kernel(a, b, c, d, own, sent):
    for i, out in enumerate((own, sent)):
        total = a[i] + b[i].astype(F32) + c[i].astype(F32) + d[i].astype(F32)
        out[...] = total.T.astype(BF)


def sum_second(parts):
    shape = parts[0].shape
    return pl.pallas_call(
        sum_second_kernel,
        in_specs=[VMEM] * 4,
        out_specs=[VMEM] * 2,
        out_shape=[jax.ShapeDtypeStruct((BLK, shape[1]), BF)] * 2,
        name="sum_second",
    )(*parts)


def gather_plane(own):
    from_before = pp1(own, 1)
    from_after = pp1(own, -1)
    from_far = pp1(own, 2)
    line = jnp.concatenate([own, from_before, from_after, from_far], axis=0)
    before = pp2(line, 1)
    after = pp2(line, -1)
    half = line.shape[0] // 2
    far_0 = pp2(before[:half], 1)
    far_1 = pp2(after[half:], -1)
    return [line, before, after, far_0, far_1]


def shards(states, loss_grad, gains, w_param, w_fixed, probes):
    grp = lax.axis_index("grp")
    zh = lax.axis_index("zh")
    mp = lax.axis_index("mp")
    place = (((grp * NX + lax.axis_index("x")) * NZ + zh) * NY + lax.axis_index("y")) * NM + mp
    tab = lax.dynamic_index_in_dim(jnp.asarray(position_table()), place, 0, keepdims=False)
    seqs, length, width = states.shape[1:]
    rows = seqs * length
    own_rows = states[0].reshape(rows, width)
    weight = float(rows * 32) ** (-0.5)

    def packed(first):
        def pick(x):
            a, b = x[:, :HEAD], x[:, HEAD:]
            return jnp.where(first, a, b), jnp.where(first, b, a)

        f0, f1 = pick(w_fixed[0])
        return jnp.concatenate(
            [f1, f0, pick(w_param[0])[0], pick(probes[0, :, 0])[0], pick(probes[0, :, 1])[0]], axis=1
        )

    mine = packed(zh == 0)
    theirs = pp_pair(packed(zh != 0))

    quarter = lax.dynamic_slice_in_dim(states[0], mp * 32, 32, axis=1)
    p1 = ppz(quarter, 1)
    m1 = ppz(quarter, -1)
    p2 = ppz(p1, 1)
    m2 = ppz(m1, -1)
    p3 = ppz(p2, 1)
    m3 = ppz(m2, -1)
    f0 = ppz(p3[0:1], 1)
    f1 = ppz(m3[1:2], -1)

    weights = gather_plane(mine) + gather_plane(theirs)

    n_a, s_a = norm_own(tab, own_rows, loss_grad.reshape(rows, width), gains)
    own_a, sent = proj_own(n_a, s_a, weights)
    n_b = norm_pair(tab, gains, (p1, p2, p3, m1, m2, m3, f0, f1))
    own_b = proj_pair(n_b, weights)

    v_b = lax.ppermute(sent, ("grp", "zh"), [(0, 3), (1, 2)])
    o_b = lax.ppermute(sent, ("grp", "zh"), [(2, 3), (3, 2)])
    got_a = lax.ppermute(own_a, "grp", [(1, 0)])
    got_b = lax.ppermute(own_b, "grp", [(0, 1)])
    keep, send = attention(weight, tab, own_a, got_a, own_b, got_b, v_b, o_b)
    got = lax.ppermute(send, "grp", [(0, 1), (1, 0)])

    far, before, after, line = [outer(tab, n_a, n_b, keep, got, g) for g in (3, 1, 2, 0)]
    r_far = pp2(far, 2)
    r_before = pp2(before, -1)
    r_after = pp2(after, 1)
    s0, s1, s2, s3 = sum_first((line, r_far, r_before, r_after))
    own, pair = sum_second((s0, pp1(s1, -1), pp1(s2, 1), pp1(s3, 2)))
    other = pp_pair(pair)
    own = own.reshape(BLK, 2, HEAD)
    other = other.reshape(BLK, 2, HEAD)
    out = jnp.concatenate([jnp.where(zh == 0, own, other), jnp.where(zh == 0, other, own)], axis=2)
    return out[None]


def solution(mesh):
    fine = Mesh(mesh.devices.reshape(2, NX, NZ, NY, NM), ("grp", "x", "zh", "y", "mp"))
    dp = ("x", "zh", "y")
    in_specs = (
        P("grp", dp, None, None),
        P(dp, None, None),
        P("grp", None),
        P("grp", dp, "mp"),
        P("grp", dp, "mp"),
        P("grp", dp, None, "mp"),
    )
    out_specs = P("grp", dp, None, "mp")
    return jax.shard_map(shards, mesh=fine, in_specs=in_specs, out_specs=out_specs, check_vma=False)
```

```python
import numpy as np
import jax
import jax.numpy as jnp
from jax import lax
from jax.experimental import pallas as pl
from jax.experimental.pallas import tpu as pltpu
from jax.sharding import Mesh, PartitionSpec as P

HEAD = 256
EPS = 1e-06
BF = jnp.bfloat16
F32 = jnp.float32
NX, NY, NZ, NM = 4, 4, 2, 4
BLK = 128
OFFS = (0, -1, 1, 2)


def position_table():
    rows = []
    for grp in range(2):
        for x in range(NX):
            for zh in range(NZ):
                for y in range(NY):
                    for mp in range(NM):
                        row = []
                        for c in range(2):
                            for o2 in OFFS:
                                for o1 in OFFS:
                                    ox, oy = (o1, o2) if grp == 0 else (o2, o1)
                                    xx, yy = (x + ox) % NX, (y + oy) % NY
                                    row.append(xx * 8 + (zh ^ c) * 4 + yy)
                        rows.append(row + [grp, mp, zh])
    return np.asarray(rows, np.int32)


def plane_perm(first, step):
    pairs = []
    for g in range(2):
        for x in range(NX):
            for y in range(NY):
                along_x = (g == 0) == first
                tx, ty = ((x + step) % NX, y) if along_x else (x, (y + step) % NY)
                pairs.append((g * 16 + x * 4 + y, g * 16 + tx * 4 + ty))
    return pairs


def pp1(v, step):
    return lax.ppermute(v, ("grp", "x", "y"), plane_perm(True, step))


def pp2(v, step):
    return lax.ppermute(v, ("grp", "x", "y"), plane_perm(False, step))


def ppz(v, step):
    return lax.ppermute(v, ("zh", "mp"), [(i, (i + step) % 8) for i in range(8)])


def pp_pair(v):
    return lax.ppermute(v, "zh", [(0, 1), (1, 0)])


SMEM = pl.BlockSpec(memory_space=pltpu.SMEM)
VMEM = pl.BlockSpec(memory_space=pltpu.VMEM)


def pack_kernel(tab, fixed, param, probe, mine, theirs):
    def put(out, head):
        own, other = slice(head * HEAD, (head + 1) * HEAD), slice((1 - head) * HEAD, (2 - head) * HEAD)
        out[:, 0:HEAD] = fixed[:, other]
        out[:, HEAD : 2 * HEAD] = fixed[:, own]
        out[:, 2 * HEAD : 3 * HEAD] = param[:, own]
        for p in range(2):
            out[:, (3 + p) * HEAD : (4 + p) * HEAD] = probe[:, p, own]

    for head in range(2):

        @pl.when(tab[34] == head)
        def _():
            put(mine, head)
            put(theirs, 1 - head)


def pack(tab, fixed, param, probe):
    return pl.pallas_call(
        pack_kernel,
        in_specs=[SMEM] + [VMEM] * 3,
        out_specs=[VMEM] * 2,
        out_shape=[jax.ShapeDtypeStruct((fixed.shape[0], 5 * HEAD), BF)] * 2,
        name="pack",
    )(tab, fixed, param, probe)


def norm_rows(tab, rows, gains, out, count):
    def chunk(i, carry):
        at = pl.ds(pl.multiple_of(i * 16, 16), 16)
        total = jnp.zeros((16, BLK), F32)
        for b in range(32):
            piece = rows[at, b * BLK : (b + 1) * BLK].astype(F32)
            total = total + piece * piece
        scale = lax.rsqrt(jnp.sum(total, axis=-1, keepdims=True) * (1.0 / (32 * BLK)) + EPS)
        for b in range(32):
            src = pl.ds(pl.multiple_of(tab[b] * BLK, BLK), BLK)
            out[at, b * BLK : (b + 1) * BLK] = (rows[at, src].astype(F32) * scale * gains[:, src]).astype(BF)
        return carry

    lax.fori_loop(0, count // 16, chunk, 0)


def norm_own_kernel(tab, rows, gains, out):
    norm_rows(tab, rows, gains, out, rows.shape[0])


def norm_own(tab, rows, gains):
    n, width = rows.shape
    step = 64
    spec = pl.BlockSpec((step, width), lambda i: (i, 0))
    return pl.pallas_call(
        norm_own_kernel,
        grid=(n // step,),
        in_specs=[SMEM, spec, pl.BlockSpec((1, width), lambda i: (0, 0))],
        out_specs=spec,
        out_shape=jax.ShapeDtypeStruct((n, width), BF),
        name="norm_own",
    )(tab, rows, gains)


def norm_pair_kernel(tab, gains, p1, p2, p3, m1, m2, m3, f0, f1, out, raw, sems):
    mp = tab[33]
    sources = {-3: (m1, m1), -2: (m2, m2), -1: (m3, m3), 0: (f0, f1), 1: (p3, p3), 2: (p2, p2), 3: (p1, p1)}

    def copies(act):
        for d, pair in sources.items():

            @pl.when((mp + d >= 0) & (mp + d < NM))
            def _():
                for s in range(2):
                    at = pl.ds(pl.multiple_of(s * 128 + (mp + d) * 32, 32), 32)
                    src = pair[s].at[s if d != 0 else 0]
                    act(pltpu.make_async_copy(src, raw.at[at], sems.at[d + 3, s]))

    copies(lambda c: c.start())
    copies(lambda c: c.wait())
    norm_rows(tab, raw, gains, out, raw.shape[0])


def norm_pair(tab, gains, pieces):
    width = gains.shape[1]
    hbm = pl.BlockSpec(memory_space=pl.ANY)
    return pl.pallas_call(
        norm_pair_kernel,
        in_specs=[SMEM, VMEM] + [hbm] * 8,
        out_specs=VMEM,
        out_shape=jax.ShapeDtypeStruct((256, width), BF),
        scratch_shapes=[pltpu.VMEM((256, width), BF), pltpu.SemaphoreType.DMA((7, 2))],
        name="norm_pair",
    )(tab, gains, *pieces)


def dots(lhs_of, weights, base):
    total = None
    for w in weights:
        k = w.shape[0]
        part = jnp.dot(lhs_of(base, k), w[...], preferred_element_type=F32)
        total = part if total is None else total + part
        base += k
    return total


def plain(ref):
    return lambda base, k: ref[:, base : base + k]


def permuted(tab, ref):
    def lhs(base, k):
        first = base // BLK
        return jnp.concatenate(
            [ref[:, pl.ds(pl.multiple_of(tab[first + i] * BLK, BLK), BLK)] for i in range(k // BLK)], axis=1
        )

    return lhs


def own_dots(tab, n, lg, weights, base, use):
    j = pl.program_id(0)
    swap = (j < 2) & (tab[32] != 0)

    @pl.when(swap)
    def _():
        use(dots(permuted(tab, lg), weights, base))

    @pl.when(jnp.logical_not(swap))
    def _():
        use(dots(plain(n), weights, base))


def whole(ref):
    return pl.BlockSpec(ref.shape, lambda j: (0, 0))


def column(ref, shift=0):
    return pl.BlockSpec((ref.shape[0], HEAD), lambda j: (0, j + shift))


def own_first_kernel(tab, n, lg, *refs):
    weights, out = refs[:-1], refs[-1]

    def use(v):
        out[...] = v

    own_dots(tab, n, lg, weights, 0, use)


def own_first(tab, n, lg, weights):
    return pl.pallas_call(
        own_first_kernel,
        grid=(5,),
        in_specs=[SMEM, whole(n), whole(lg)] + [column(w) for w in weights],
        out_specs=pl.BlockSpec((n.shape[0], HEAD), lambda j: (0, j)),
        out_shape=jax.ShapeDtypeStruct((n.shape[0], 5 * HEAD), F32),
        name="own_first",
    )(tab, n, lg, *weights)


def pair_first_kernel(n, *refs):
    refs[-1][...] = dots(plain(n), refs[:-1], 0)


def pair_first(n, weights):
    return pl.pallas_call(
        pair_first_kernel,
        grid=(3,),
        in_specs=[whole(n)] + [column(w, 2) for w in weights],
        out_specs=pl.BlockSpec((n.shape[0], HEAD), lambda j: (0, j)),
        out_shape=jax.ShapeDtypeStruct((n.shape[0], 3 * HEAD), F32),
        name="pair_first",
    )(n, *weights)


def middle_kernel(base, tab, n, lg, n_b, acc_a, acc_b, *refs):
    weights, (out_a, out_b) = refs[:-2], refs[-2:]

    def use(v):
        out_a[...] = acc_a[...] + v

    own_dots(tab, n, lg, weights, base, use)

    @pl.when(pl.program_id(0) >= 2)
    def _():
        out_b[...] = acc_b[...] + dots(plain(n_b), weights, base)


def late(n):
    return pl.BlockSpec((n.shape[0], HEAD), lambda j: (0, jnp.maximum(j - 2, 0)))


def middle(tab, n, lg, n_b, acc_a, acc_b, weights, base):
    return pl.pallas_call(
        lambda *refs: middle_kernel(base, *refs),
        grid=(5,),
        in_specs=[SMEM, whole(n), whole(lg), whole(n_b), column(acc_a), late(n)] + [column(w) for w in weights],
        out_specs=[column(acc_a), late(n)],
        out_shape=[jax.ShapeDtypeStruct(acc_a.shape, F32), jax.ShapeDtypeStruct(acc_b.shape, F32)],
        name="middle",
    )(tab, n, lg, n_b, acc_a, acc_b, *weights)


def last_kernel(base, tab, n, lg, n_b, acc_a, acc_b, *refs):
    weights, (sent, out_a, out_b) = refs[:-3], refs[-3:]
    j = pl.program_id(0)

    def use(v):
        v = (acc_a[...] + v).astype(BF)

        @pl.when(j == 0)
        def _():
            sent[...] = v

        @pl.when(j != 0)
        def _():
            out_a[...] = v

    own_dots(tab, n, lg, weights, base, use)

    @pl.when(j >= 2)
    def _():
        out_b[...] = (acc_b[...] + dots(plain(n_b), weights, base)).astype(BF)


def last(tab, n, lg, n_b, acc_a, acc_b, weights, base):
    rows = n.shape[0]
    return pl.pallas_call(
        lambda *refs: last_kernel(base, *refs),
        grid=(5,),
        in_specs=[SMEM, whole(n), whole(lg), whole(n_b), column(acc_a), late(n)] + [column(w) for w in weights],
        out_specs=[
            pl.BlockSpec((rows, HEAD), lambda j: (0, 0)),
            pl.BlockSpec((rows, HEAD), lambda j: (0, jnp.maximum(j - 1, 0))),
            late(n),
        ],
        out_shape=[jax.ShapeDtypeStruct((rows, k * HEAD), BF) for k in (1, 4, 3)],
        name="last",
    )(tab, n, lg, n_b, acc_a, acc_b, *weights)


NT = (((1,), (1,)), ((), ()))
TN = (((0,), (0,)), ((), ()))


def curvature(q, k, v, o, tq, tk, weight):
    dot = lambda a, b, dims: lax.dot_general(a, b, dims, preferred_element_type=F32)
    scores = dot(q, k, NT)
    top = jnp.max(scores, axis=-1, keepdims=True)
    e = jnp.exp(scores - top)
    probs = e / jnp.sum(e, axis=-1, keepdims=True)
    mixing = dot(o, v, NT)
    centred = mixing - jnp.sum(probs * mixing, axis=-1, keepdims=True)
    grad = probs * centred
    grad_b = grad.astype(BF)
    dqs, dks = [], []
    for p in range(2):
        t_scores = dot(tq[p], k, NT) + dot(q, tk[p], NT)
        t_probs = probs * (t_scores - jnp.sum(probs * t_scores, axis=-1, keepdims=True))
        t_mean = jnp.sum(t_probs * mixing, axis=-1, keepdims=True)
        t_grad = t_probs * centred - probs * t_mean
        t_b = t_grad.astype(BF)
        dq = jnp.dot(t_b, k, preferred_element_type=F32) + jnp.dot(grad_b, tk[p], preferred_element_type=F32)
        dk = dot(t_b, q, TN) + dot(grad_b, tq[p], TN)
        dqs.append((dq * weight).T.astype(BF))
        dks.append((dk * weight).T.astype(BF))
    return dqs, dks


def attention_kernel(weight, tab, own_a, got_a, own_b, got_b, v_b, o_b, keep, send):
    def tile(ref, s, j):
        return ref[s * 128 : (s + 1) * 128, j * HEAD : (j + 1) * HEAD]

    def both(key_ref, query_ref, value_of, outgrad_of, base, key_out, query_out):
        for s in range(2):
            dqs, dks = curvature(
                tile(query_ref, s, base),
                tile(key_ref, s, base),
                value_of(s),
                outgrad_of(s),
                [tile(query_ref, s, base + 1 + p) for p in range(2)],
                [tile(key_ref, s, base + 1 + p) for p in range(2)],
                weight,
            )
            for p in range(2):
                query_out[p * HEAD : (p + 1) * HEAD, s * 128 : (s + 1) * 128] = dqs[p]
                key_out[p * HEAD : (p + 1) * HEAD, s * 128 : (s + 1) * 128] = dks[p]

    @pl.when(tab[32] == 0)
    def _():
        both(own_a, got_a, lambda s: tile(own_a, s, 0), lambda s: tile(got_a, s, 0), 1, keep, send)

    @pl.when(tab[32] != 0)
    def _():
        both(got_b, own_b, lambda s: tile(v_b, s, 0), lambda s: tile(o_b, s, 0), 0, send, keep)


def attention(weight, *args):
    return pl.pallas_call(
        lambda *refs: attention_kernel(weight, *refs),
        in_specs=[SMEM] + [VMEM] * 6,
        out_specs=[VMEM, VMEM],
        out_shape=[jax.ShapeDtypeStruct((2 * HEAD, 256), BF)] * 2,
        name="attention",
    )(*args)


def outer_kernel(tab, n_a, n_b, keep, got, out):
    @pl.when(tab[32] == 0)
    def _():
        out[0] = (
            jnp.dot(keep[...], n_a[...], preferred_element_type=F32)
            + jnp.dot(got[...], n_b[...], preferred_element_type=F32)
        ).astype(BF)

    @pl.when(tab[32] != 0)
    def _():
        out[0] = (
            jnp.dot(got[...], n_a[...], preferred_element_type=F32)
            + jnp.dot(keep[...], n_b[...], preferred_element_type=F32)
        ).astype(BF)


def outer(tab, n_a, n_b, keep, got, group):
    rows = n_a.shape[0]
    wide = pl.BlockSpec((rows, 4 * BLK), lambda c: (0, c * 4 + group))
    small = pl.BlockSpec((2 * HEAD, rows), lambda c: (0, 0))
    return pl.pallas_call(
        outer_kernel,
        grid=(2,),
        in_specs=[SMEM, wide, wide, small, small],
        out_specs=pl.BlockSpec((1, 2 * HEAD, 4 * BLK), lambda c: (c, 0, 0)),
        out_shape=jax.ShapeDtypeStruct((2, 2 * HEAD, 4 * BLK), BF),
        name="outer",
    )(tab, n_a, n_b, keep, got)


def sum_first_kernel(a, b, c, d, *outs):
    total = a[...].astype(F32) + b[...].astype(F32) + c[...].astype(F32) + d[...].astype(F32)
    for i, out in enumerate(outs):
        out[...] = total[:, :, i * BLK : (i + 1) * BLK].astype(out.dtype)


def sum_first(parts):
    shape = parts[0].shape
    step = 128
    spec = pl.BlockSpec((1, step, shape[2]), lambda c, i: (c, i, 0))
    return pl.pallas_call(
        sum_first_kernel,
        grid=(shape[0], shape[1] // step),
        in_specs=[spec] * 4,
        out_specs=[pl.BlockSpec((1, step, BLK), lambda c, i: (c, i, 0))] * 4,
        out_shape=[jax.ShapeDtypeStruct((shape[0], shape[1], BLK), F32 if i == 0 else BF) for i in range(4)],
        name="sum_first",
    )(*parts)


def sum_second_kernel(a, b, c, d, own, sent):
    for i, out in enumerate((own, sent)):
        total = a[i] + b[i].astype(F32) + c[i].astype(F32) + d[i].astype(F32)
        out[...] = total.T.astype(BF)


def sum_second(parts):
    shape = parts[0].shape
    return pl.pallas_call(
        sum_second_kernel,
        in_specs=[VMEM] * 4,
        out_specs=[VMEM] * 2,
        out_shape=[jax.ShapeDtypeStruct((BLK, shape[1]), BF)] * 2,
        name="sum_second",
    )(*parts)


def gather_line(own):
    far = pp1(own, 2)
    before = pp1(own, 1)
    after = pp1(own, -1)
    return jnp.concatenate([own, before, after, far], axis=0)


def gather_rest(line):
    before = pp2(line, 1)
    after = pp2(line, -1)
    half = line.shape[0] // 2
    far_0 = pp2(before[:half], 1)
    far_1 = pp2(after[half:], -1)
    return [before, after], [far_0, far_1]


def body(states, loss_grad, gains, w_param, w_fixed, probes):
    grp = lax.axis_index("grp")
    zh = lax.axis_index("zh")
    mp = lax.axis_index("mp")
    place = (((grp * NX + lax.axis_index("x")) * NZ + zh) * NY + lax.axis_index("y")) * NM + mp
    tab = lax.dynamic_index_in_dim(jnp.asarray(position_table()), place, 0, keepdims=False)
    seqs, length, width = states.shape[1:]
    rows = seqs * length
    own_rows = states[0].reshape(rows, width)
    lg = loss_grad.reshape(rows, width)
    weight = float(rows * 32) ** (-0.5)

    quarter = lax.dynamic_slice_in_dim(states[0], mp * 32, 32, axis=1)
    p1 = ppz(quarter, 1)
    m1 = ppz(quarter, -1)
    p2 = ppz(p1, 1)
    m2 = ppz(m1, -1)
    p3 = ppz(p2, 1)
    m3 = ppz(m2, -1)
    f0 = ppz(p3[0:1], 1)
    f1 = ppz(m3[1:2], -1)

    mine, theirs = pack(tab, w_fixed[0], w_param[0], probes[0])
    theirs = pp_pair(theirs)
    line1 = gather_line(mine)
    near1, far1 = gather_rest(line1)
    line2 = gather_line(theirs)
    near2, far2 = gather_rest(line2)
    first = [line1] + near1 + far1
    half = 16 * BLK
    n_a = norm_own(tab, own_rows, gains)
    acc_a = own_first(tab, n_a, lg, first)
    n_b = norm_pair(tab, gains, (p1, p2, p3, m1, m2, m3, f0, f1))
    acc_b = pair_first(n_b, first)
    acc_a, acc_b = middle(tab, n_a, lg, n_b, acc_a, acc_b, [line2] + near2, half)
    sent, own_a, own_b = last(tab, n_a, lg, n_b, acc_a, acc_b, far2, half + 12 * BLK)

    v_b = lax.ppermute(sent, ("grp", "zh"), [(0, 3), (1, 2)])
    o_b = lax.ppermute(sent, ("grp", "zh"), [(2, 3), (3, 2)])
    got_a = lax.ppermute(own_a, "grp", [(1, 0)])
    got_b = lax.ppermute(own_b, "grp", [(0, 1)])
    keep, send = attention(weight, tab, own_a, got_a, own_b, got_b, v_b, o_b)
    got = lax.ppermute(send, "grp", [(0, 1), (1, 0)])

    far, before, after, line = [outer(tab, n_a, n_b, keep, got, g) for g in (3, 1, 2, 0)]
    r_far = pp2(far, 2)
    r_before = pp2(before, -1)
    r_after = pp2(after, 1)
    s0, s1, s2, s3 = sum_first((line, r_far, r_before, r_after))
    own, pair = sum_second((s0, pp1(s1, -1), pp1(s2, 1), pp1(s3, 2)))
    other = pp_pair(pair)
    own = own.reshape(BLK, 2, HEAD)
    other = other.reshape(BLK, 2, HEAD)
    out = jnp.concatenate([jnp.where(zh == 0, own, other), jnp.where(zh == 0, other, own)], axis=2)
    return out[None]


def solution(mesh):
    fine = Mesh(mesh.devices.reshape(2, NX, NZ, NY, NM), ("grp", "x", "zh", "y", "mp"))
    dp = ("x", "zh", "y")
    in_specs = (
        P("grp", dp, None, None),
        P(dp, None, None),
        P("grp", None),
        P("grp", dp, "mp"),
        P("grp", dp, "mp"),
        P("grp", dp, None, "mp"),
    )
    out_specs = P("grp", dp, None, "mp")
    return jax.shard_map(body, mesh=fine, in_specs=in_specs, out_specs=out_specs, check_vma=False)
```
